256 devices in a mesh: side: 2 (over x_lo), slab: 128 (over y, z, x_hi, core).
Axes of the slice: x: 4 (x_hi: 2, x_lo: 2; x = x_hi * 2 + x_lo), y: 4, z: 8, core: 2. Of those that a mesh axis runs over, the one named last changes fastest.
Arguments:
- source: float32 [2, 512, 256, 256], P('side', 'slab'), may hold values from -6 to 6
- conduct: float32 [2, 512, 256, 256], P('side', 'slab'), may hold values from 0.2 to 5
- reaction: float32 [2, 512, 256, 256], P('side', 'slab'), may hold values from 0.05 to 2
- robin_gain: float32 [2, 512, 256], P('side', 'slab'), may hold values from 0.5 to 4
- mortar: float32 [2, 1024, 128, 128], P('side', 'slab'), may hold values from -0.5 to 0.5
- dst_part: int32 [2, 1024], P('side', 'slab'), may hold values from 0 to 127, as said below
- dst_slot: int32 [2, 1024], P('side', 'slab'), may hold values from 0 to 7
Outputs:
- solution: float32 [2, 512, 256, 256], P('side', 'slab')
- incoming: float32 [2, 1024, 128], P('side', 'slab')
The draws below stay inside these ranges and needn't reach their ends.
Inputs may be any that keep to these rules, and one draw needn't show every extreme that they name: For each side, dst_part and dst_slot map the 1024 blocks one to one onto the 1024 blocks of the other side. Each partition sends its blocks to four partitions of the other side, at four distinct offsets of the partition index (modulo 128), one of which is 64, with four block counts of 1 or more that are the same for all partitions of that side; no partition sends more than 3 blocks to one partition, and every draw has such pairs with exactly 3.
All inputs are finite; a program needn't handle non-finite values.
Results may differ from the reference program's by a relative error of at most 0.0001.
Values sent between devices are 32-bit elements; how exact they have to be, the bound alone decides.
No kernel may reach another device: no remote copies, remote signals or barrier semaphores. Data moves between devices by JAX's collectives and lax.ppermute only.
A program may use at most 64 MiB of HBM per device.

```python
import math
import jax
import jax.numpy as jnp
from jax import lax

NY = 256
NZ = 256
MB = 128
DEGREE = 4
ROBIN = 2
NBLK = 8
CAP = 3
NPART = 128
NX = 512
NB_ALL = 1024


def build_routes(key):
    part_rows = []
    slot_rows = []
    remainder = NBLK - CAP
    second_low = max(1, remainder - 2 * CAP)
    second_high = min(CAP, remainder - 2)
    half_offset = NPART // 2
    for side_index in range(2):
        subkeys = jax.random.split(jax.random.fold_in(key, 11 + side_index), 6)
        others = jax.random.permutation(subkeys[0], NPART - 1)[:3].astype(jnp.int32)
        others = others + (others >= half_offset).astype(jnp.int32)
        shifts = jnp.concatenate([jnp.array([half_offset], jnp.int32), others])
        second = jax.random.randint(subkeys[1], (), second_low, second_high + 1).astype(jnp.int32)
        third_low = jnp.maximum(1, remainder - second - CAP)
        third_high = jnp.minimum(CAP, remainder - second - 1)
        third = jax.random.randint(subkeys[2], (), third_low, third_high + 1).astype(jnp.int32)
        fourth = (remainder - second - third).astype(jnp.int32)
        group_sizes = jnp.stack([jnp.int32(CAP), second, third, fourth])
        group_sizes = group_sizes[jax.random.permutation(subkeys[3], 4)]
        group_ends = jnp.cumsum(group_sizes).astype(jnp.int32)
        source_keys = jax.random.split(subkeys[4], NPART)
        position = jax.vmap(lambda one_key: jax.random.permutation(one_key, NBLK))(source_keys).astype(jnp.int32)
        receive_keys = jax.random.split(subkeys[5], NPART)
        receive_order = jax.vmap(lambda one_key: jax.random.permutation(one_key, NBLK))(receive_keys).astype(jnp.int32)
        group_of = jnp.sum((position[:, :, None] >= group_ends[None, None, :]).astype(jnp.int32), axis=-1)
        sender = jnp.arange(NPART, dtype=jnp.int32)[:, None]
        receiver = (sender + shifts[group_of]) % NPART
        slot_at = receive_order[receiver, position]
        part_rows.append(receiver.reshape(NB_ALL))
        slot_rows.append(slot_at.reshape(NB_ALL))
    return (jnp.stack(part_rows).astype(jnp.int32), jnp.stack(slot_rows).astype(jnp.int32))


def draw_dst_part(key, part):
    return build_routes(jax.random.fold_in(key, 7))[0]


def draw_dst_slot(key, part):
    return build_routes(jax.random.fold_in(key, 7))[1]


def shard_levels(own_key, dims, cuts, least, high):
    loudness, own = 1.0, jax.random.fold_in(own_key, 6)
    for axis_at, blocks in cuts:
        heights = jnp.exp(jax.random.uniform(jax.random.fold_in(own, axis_at), (blocks,), jnp.float32, least / len(cuts), high / len(cuts)))
        loudness = loudness * jnp.repeat(heights, dims[axis_at] // blocks).reshape([-1 if axis == axis_at else 1 for axis in range(len(dims))])
    return loudness


def gaussian(key, shape, deviation, reach, shards=(), held_as=jnp.bfloat16):
    entries = deviation * jax.random.normal(key, shape, jnp.float32)
    if shards:
        entries = entries * shard_levels(key, shape, shards, -0.22, 0.18)
    return jnp.clip(entries, -reach, reach).astype(held_as)


def setup_inputs(seed: int = 0) -> dict:
    keys = jax.random.split(jax.random.key(seed), 8)
    source = gaussian(keys[0], (2, NX, NY, NZ), 1.0, 6.0, ((0, 2), (1, 128)), jnp.float32)
    conduct = jnp.clip(jnp.exp(math.log(5.0) - 3.218876 * jax.random.uniform(keys[1], (2, NX, NY, NZ), jnp.float32) ** shard_levels(keys[1], (2, NX, NY, NZ), ((0, 2), (1, 128)), -0.2, 0.2)), 0.2, 5.0)
    reaction = jnp.clip(jnp.exp(math.log(2.0) - 3.6888794 * jax.random.uniform(keys[2], (2, NX, NY, NZ), jnp.float32) ** shard_levels(keys[2], (2, NX, NY, NZ), ((0, 2), (1, 128)), -0.2, 0.2)), 0.05, 2.0)
    robin_gain = jnp.clip(jnp.exp(math.log(4.0) - 2.0794415 * jax.random.uniform(keys[3], (2, NX, NY), jnp.float32) ** shard_levels(keys[3], (2, NX, NY), ((0, 2), (1, 128)), -0.2, 0.2)), 0.5, 4.0)
    mortar = gaussian(keys[4], (2, NB_ALL, MB, MB), MB ** -0.5, 0.5, ((0, 2), (1, 128)), jnp.float32)
    dst_part = draw_dst_part(jax.random.fold_in(keys[7], 71), 0)
    dst_slot = draw_dst_slot(jax.random.fold_in(keys[7], 71), 0)
    return {"source": source, "conduct": conduct, "reaction": reaction, "robin_gain": robin_gain, "mortar": mortar, "dst_part": dst_part, "dst_slot": dst_slot}


cheb_low = 0.1
cheb_high = 2.0


def operate(current, conduct, reaction, robin_gain):
    padded = jnp.pad(current, 1)
    beside_all = padded[2:, 1:-1, 1:-1] + padded[:-2, 1:-1, 1:-1]
    beside_all = beside_all + padded[1:-1, 2:, 1:-1] + padded[1:-1, :-2, 1:-1]
    beside_all = beside_all + padded[1:-1, 1:-1, 2:] + padded[1:-1, 1:-1, :-2]
    applied = conduct * (6.0 * current - beside_all) + reaction * current
    return applied.at[:, :, -1].add(robin_gain * current[:, :, -1])


def chebyshev(start, right_side, conduct, reaction, robin_gain, diagonal):
    centre = (cheb_high + cheb_low) / 2.0
    half_width = (cheb_high - cheb_low) / 2.0
    ratio_cheb = centre / half_width
    weight_old = 1.0 / ratio_cheb
    current = start
    step_dir = jnp.zeros_like(start)
    for sweep_index in range(DEGREE):
        residual = right_side - operate(current, conduct, reaction, robin_gain)
        if sweep_index == 0:
            step_dir = residual / diagonal / centre
        else:
            weight_new = 1.0 / (2.0 * ratio_cheb - weight_old)
            step_dir = weight_new * weight_old * step_dir + (2.0 * weight_new / half_width) * (residual / diagonal)
            weight_old = weight_new
        current = current + step_dir
    return current


def robin_datum(current, conduct, robin_gain):
    top_layer = current[:, :, -1]
    below_layer = current[:, :, -2]
    return robin_gain * top_layer - conduct[:, :, -1] * (top_layer - below_layer)


def reference(source, conduct, reaction, robin_gain, mortar, dst_part, dst_slot):
    diagonals = []
    for side_index in range(2):
        diagonal = 6.0 * conduct[side_index] + reaction[side_index]
        diagonals.append(diagonal.at[:, :, -1].add(robin_gain[side_index]))

    def solve(side_index, start, arrived):
        right_side = source[side_index].at[:, :, -1].add(arrived.reshape(NX, NY))
        return chebyshev(start, right_side, conduct[side_index], reaction[side_index], robin_gain[side_index], diagonals[side_index])

    empty = jnp.zeros((NB_ALL, MB), jnp.float32)
    fields = [solve(side_index, jnp.zeros((NX, NY, NZ), jnp.float32), empty) for side_index in range(2)]
    arrived_all = [empty, empty]
    for robin_step in range(ROBIN):
        received = []
        for side_index in range(2):
            datum = robin_datum(fields[side_index], conduct[side_index], robin_gain[side_index]).reshape(NB_ALL, MB)
            projected = jnp.einsum("gjk,gk->gj", mortar[side_index], datum, precision=lax.Precision.HIGHEST)
            target = dst_part[side_index] * NBLK + dst_slot[side_index]
            received.append(jnp.zeros((NB_ALL, MB), jnp.float32).at[target].set(projected))
        arrived_all = [received[1], received[0]]
        fields = [solve(side_index, fields[side_index], arrived_all[side_index]) for side_index in range(2)]
    return jnp.stack(fields), jnp.stack(arrived_all)
```

```python
import jax
import jax.numpy as jnp
from jax import lax
from jax.experimental import pallas as pl
from jax.experimental.pallas import tpu as pltpu
from jax.sharding import PartitionSpec as P

DEGREE = 4
ROBIN = 2
CAP = 3
HALO = DEGREE - 1

cheb_low = 0.1
cheb_high = 2.0

AXES = ("side", "slab")
VMEM = pl.BlockSpec(memory_space=pltpu.VMEM)
SMEM = pl.BlockSpec(memory_space=pltpu.SMEM)


def cheb_weights():
    centre = (cheb_high + cheb_low) / 2.0
    half_width = (cheb_high - cheb_low) / 2.0
    ratio = centre / half_width
    weight_old = half_width / centre
    weights = [(0.0, 1.0 / centre)]
    for _ in range(DEGREE - 1):
        weight_new = 1.0 / (2.0 * ratio - weight_old)
        weights.append((weight_new * weight_old, 2.0 * weight_new / half_width))
        weight_old = weight_new
    return weights


def prepare_kernel(
    par_ref, src_ref, con_ref, rea_ref, gain_ref, beta_ref, gamma_ref, inter_ref, same_ref, face_ref
):
    rows, ny, nz = src_ref.shape
    lanes = 128
    tiles = nz // lanes
    per_row = tiles * ny
    flip = par_ref[0] == 0
    chunk = lanes
    last_lane = lax.broadcasted_iota(jnp.int32, (chunk, lanes), 1) == lanes - 1
    base = HALO * per_row
    for row in range(rows):
        held = jnp.where(flip, rows - 1 - row, row)
        for tile in range(tiles):
            for part in range(ny // chunk):
                ys = pl.ds(part * chunk, chunk)
                zs = pl.ds(tile * lanes, lanes)
                con = con_ref[held, ys, zs]
                diag = 6.0 * con + rea_ref[held, ys, zs]
                if tile == tiles - 1:
                    gains = gain_ref[held, :, ys]
                    column = jnp.broadcast_to(gains, (chunk, chunk)).T
                    diag = diag + jnp.where(last_lane, column, 0.0)
                inverse = 1.0 / diag
                beta = src_ref[held, ys, zs] * inverse
                gamma = con * inverse
                at = tile * ny + part * chunk
                beta_ref[row, pl.ds(at, chunk), :] = beta
                gamma_ref[row, pl.ds(at, chunk), :] = gamma
                if row >= rows - HALO:
                    to = (row - (rows - HALO)) * per_row + at
                    inter_ref[pl.ds(to, chunk), :] = beta
                    inter_ref[pl.ds(base + to, chunk), :] = gamma
                if row < HALO:
                    to = row * per_row + at
                    same_ref[pl.ds(to, chunk), :] = beta
                    same_ref[pl.ds(base + to, chunk), :] = gamma
                if tile == tiles - 1:
                    block = row * (ny // chunk) + part
                    inverse_top = inverse.T[lanes - 1 :, :]
                    con_top = con.T[lanes - 1 :, :]
                    face_ref[0, pl.ds(block, 1), :] = con_top
                    face_ref[1, pl.ds(block, 1), :] = gains
                    inter_ref[pl.ds(2 * base + block, 1), :] = inverse_top
                    same_ref[pl.ds(2 * base + block, 1), :] = inverse_top


def solve_kernel(first, last, *refs):
    refs = list(refs)
    if last:
        par_ref = refs.pop(0)
    beta_ref, gamma_ref, inter_ref, same_ref = refs[:4]
    refs = refs[4:]
    if not first:
        x_ref, x_inter_ref, x_same_ref, inv_ref, add_ref, add_inter_ref, add_same_ref = refs[:7]
        refs = refs[7:]
    out_ref = refs.pop(0)
    inc_ref = refs.pop(0) if last else None
    field, step, lift = refs
    rows = beta_ref.shape[0]
    lanes = 128
    tiles = 2
    ny = beta_ref.shape[1] // tiles
    per_row = tiles * ny
    pad = 8
    base = HALO * per_row
    chunk = 64
    parts = ny // chunk
    halves = ny // lanes
    weights = cheb_weights()
    lane = lax.broadcasted_iota(jnp.int32, (chunk, lanes), 1)
    first_lane, last_lane = lane == 0, lane == lanes - 1

    def static(which, row, at):
        if 0 <= row < rows:
            return (beta_ref, gamma_ref)[which][row, pl.ds(at, chunk), :]
        if row >= rows:
            ref, line = inter_ref, HALO + rows - 1 - row
        else:
            ref, line = same_ref, -1 - row
        return ref[pl.ds(which * base + line * per_row + at, chunk), :]

    zero = jnp.zeros((pad, lanes), jnp.float32)
    for buffer in range(2):
        for row in range(field.shape[1]):
            for tile in range(tiles):
                field[buffer, row, tile, pl.ds(0, pad), :] = zero
                field[buffer, row, tile, pl.ds(pad + ny, pad), :] = zero
    if not first:
        for row in range(-rows, 2 * rows):
            if 0 <= row < rows:
                ref, line = x_ref, row
            elif row >= rows:
                ref, line = x_inter_ref, 2 * rows - 1 - row
            else:
                ref, line = x_same_ref, -1 - row
            for tile in range(tiles):
                field[0, row + rows, tile, pl.ds(pad, ny), :] = ref[line, pl.ds(tile * ny, ny), :]
        wide = lax.broadcasted_iota(jnp.int32, (lanes, lanes), 1) == lanes - 1
        for row in range(-HALO, rows + HALO):
            if 0 <= row < rows:
                got, scale, at, line = add_ref, inv_ref, 0, row
            elif row >= rows:
                got, scale, at, line = add_inter_ref, inter_ref, 2 * base, 2 * rows - 1 - row
            else:
                got, scale, at, line = add_same_ref, same_ref, 2 * base, -1 - row
            for half in range(halves):
                block = line * halves + half
                term = got[pl.ds(block, 1), :] * scale[pl.ds(at + block, 1), :]
                column = jnp.broadcast_to(term, (lanes, lanes)).T
                lift[row + HALO, pl.ds(half * lanes, lanes), :] = jnp.where(wide, column, 0.0)

    for sweep in range(DEGREE):
        reach = HALO - sweep
        now, later = sweep % 2, (sweep + 1) % 2
        for row in range(-reach, rows + reach):

            def body(part, carry, row=row, sweep=sweep, now=now, later=later):
                y0 = pl.multiple_of(part * chunk, chunk)
                keep, gain = weights[sweep]
                here = row + rows
                if first and sweep == 0:
                    for tile in range(tiles):
                        new = gain * static(0, row, tile * ny + y0)
                        step[row + HALO, tile, pl.ds(y0, chunk), :] = new
                        field[later, here, tile, pl.ds(pad + y0, chunk), :] = new
                    return carry
                centre = [field[now, here, t, pl.ds(pad + y0, chunk), :] for t in range(tiles)]
                ahead = [pltpu.roll(c, lanes - 1, 1) for c in centre]
                behind = [pltpu.roll(c, 1, 1) for c in centre]
                for tile in range(tiles):
                    x = centre[tile]
                    beside = field[now, here + 1, tile, pl.ds(pad + y0, chunk), :]
                    beside = beside + field[now, here - 1, tile, pl.ds(pad + y0, chunk), :]
                    beside = beside + field[now, here, tile, pl.ds(pad + y0 + 1, chunk), :]
                    beside = beside + field[now, here, tile, pl.ds(pad + y0 - 1, chunk), :]
                    above = ahead[tile + 1] if tile + 1 < tiles else 0.0
                    below = behind[tile - 1] if tile > 0 else 0.0
                    beside = beside + jnp.where(last_lane, above, ahead[tile])
                    beside = beside + jnp.where(first_lane, below, behind[tile])
                    beta = static(0, row, tile * ny + y0)
                    if not first and tile == tiles - 1:
                        beta = beta + lift[row + HALO, pl.ds(y0, chunk), :]
                    scaled = beta - x + static(1, row, tile * ny + y0) * beside
                    new = gain * scaled
                    if sweep > 0:
                        new = new + keep * step[row + HALO, tile, pl.ds(y0, chunk), :]
                    if sweep < DEGREE - 1:
                        step[row + HALO, tile, pl.ds(y0, chunk), :] = new
                        field[later, here, tile, pl.ds(pad + y0, chunk), :] = x + new
                    elif last:
                        line = jnp.where(par_ref[0] == 0, rows - 1 - row, row)
                        out_ref[line, pl.ds(y0, chunk), pl.ds(tile * lanes, lanes)] = x + new
                    else:
                        out_ref[row, pl.ds(tile * ny + y0, chunk), :] = x + new
                return carry

            lax.fori_loop(0, parts, body, 0, unroll=True)
    if last:
        for row in range(rows):
            line = jnp.where(par_ref[0] == 0, rows - 1 - row, row)
            for half in range(halves):
                inc_ref[pl.ds(line * halves + half, 1), :] = add_ref[pl.ds(row * halves + half, 1), :]


def project_kernel(par_ref, to_ref, x_ref, face_ref, mortar_ref, send_ref, datum):
    rows = x_ref.shape[0]
    lanes = 128
    ny = x_ref.shape[1] // 2
    halves = ny // lanes
    blocks = rows * halves
    flip = par_ref[0] == 0
    send_ref[...] = jnp.zeros_like(send_ref)
    for row in range(rows):
        line = jnp.where(flip, rows - 1 - row, row)
        for half in range(halves):
            turned = x_ref[row, pl.ds(ny + half * lanes, lanes), :].T
            top = turned[lanes - 1 :, :]
            below = turned[lanes - 2 : lanes - 1, :]
            held = pl.ds(row * halves + half, 1)
            value = face_ref[1, held, :] * top - face_ref[0, held, :] * (top - below)
            datum[pl.ds(line * halves + half, 1), :] = value
    data = datum[...]
    for block in range(blocks):
        product = lax.dot_general(
            data,
            mortar_ref[block],
            (((1,), (1,)), ((), ())),
            precision=lax.Precision.HIGHEST,
            preferred_element_type=jnp.float32,
        )
        send_ref[pl.ds(to_ref[block], 1), :] = product[block : block + 1, :]


def place_kernel(par_ref, from_ref, got_ref, out_ref):
    blocks = out_ref.shape[0]
    halves = 2
    rows = blocks // halves
    flip = par_ref[0] == 0
    for row in range(rows):
        line = jnp.where(flip, rows - 1 - row, row)
        for half in range(halves):
            at = from_ref[line * halves + half]
            out_ref[pl.ds(row * halves + half, 1), :] = got_ref[pl.ds(at, 1), :]


def routes(count, swap_sides):
    same, inter = [], []
    for side in range(2):
        other = (1 - side if swap_sides else side) * count
        for low in range(count):
            me = side * count + low
            same.append((me, other + (low ^ 1)))
            near = low + 1 if low % 2 else low - 1
            if 0 <= near < count:
                inter.append((me, other + near))
    return inter, same


def on_device(source, conduct, reaction, robin_gain, mortar, dst_part, dst_slot):
    source, conduct, reaction, robin_gain = source[0], conduct[0], reaction[0], robin_gain[0]
    mortar, dst_part, dst_slot = mortar[0], dst_part[0], dst_slot[0]
    rows, ny, nz = source.shape
    blocks, lanes = mortar.shape[:2]
    count = lax.axis_size("slab")
    per_row = ny * nz // lanes
    parity = (lax.axis_index("slab") % 2).astype(jnp.int32).reshape(1)
    f32 = jnp.float32
    inter_route, same_route = routes(count, False)

    def exchange(inter, same):
        return lax.ppermute(inter, AXES, inter_route), lax.ppermute(same, AXES, same_route)

    rank = jnp.sum(
        jnp.tril(dst_part[:, None] == dst_part[None, :], -1).astype(jnp.int32), axis=1
    )
    to = dst_part * CAP + rank
    mine = (dst_part[:, None] == jnp.arange(count)[None, :])[:, :, None] & (
        rank[:, None] == jnp.arange(lanes)[None, :]
    )[:, None, :]
    table = jnp.sum(jnp.where(mine, dst_slot[:, None, None] + 1, 0), axis=0)
    table = lax.all_to_all(table, "slab", 0, 0, tiled=True)
    origin = jnp.arange(count)[:, None] * CAP + jnp.arange(lanes)[None, :]
    hit = table[None] == (jnp.arange(blocks) + 1)[:, None, None]
    origin = jnp.sum(jnp.where(hit, origin[None], 0), axis=(1, 2)).astype(jnp.int32)

    cells = jax.ShapeDtypeStruct((rows, per_row, lanes), f32)
    packed = jax.ShapeDtypeStruct((2 * HALO * per_row + blocks, lanes), f32)
    face = jax.ShapeDtypeStruct((blocks, lanes), f32)
    beta, gamma, inter, same, faces = pl.pallas_call(
        prepare_kernel,
        out_shape=(cells, cells, packed, packed, jax.ShapeDtypeStruct((2, blocks, lanes), f32)),
        in_specs=[SMEM] + [VMEM] * 4,
        out_specs=(VMEM,) * 5,
        name="prepare",
    )(parity, source, conduct, reaction, robin_gain[:, None, :])
    inverse = inter[2 * HALO * per_row :]
    inter, same = exchange(inter, same)

    def solve(first, last, *operands):
        scratch = [
            pltpu.VMEM((2, 3 * rows, 2, ny + 16, lanes), f32),
            pltpu.VMEM((rows + 2 * HALO, 2, ny, lanes), f32),
            pltpu.VMEM((rows + 2 * HALO, ny, lanes), f32),
        ]
        if last:
            out_shape = (jax.ShapeDtypeStruct((rows, ny, nz), f32), face)
            out_specs, lead, lead_specs = (VMEM, VMEM), (parity,), [SMEM]
        else:
            out_shape, out_specs, lead, lead_specs = cells, VMEM, (), []
        operands = (beta, gamma, inter, same) + operands
        return pl.pallas_call(
            lambda *refs: solve_kernel(first, last, *refs),
            out_shape=out_shape,
            in_specs=lead_specs + [VMEM] * len(operands),
            out_specs=out_specs,
            scratch_shapes=scratch,
            name="solve",
        )(*lead, *operands)

    cross_inter, cross_same = routes(count, True)
    cross = [(i, (i + count) % (2 * count)) for i in range(2 * count)]
    current = solve(True, False)
    for robin_step in range(ROBIN):
        x_inter, x_same = exchange(current, current)
        send = pl.pallas_call(
            project_kernel,
            out_shape=jax.ShapeDtypeStruct((count * CAP, lanes), f32),
            in_specs=[SMEM, SMEM, VMEM, VMEM, VMEM],
            out_specs=VMEM,
            scratch_shapes=[pltpu.VMEM((blocks, lanes), f32)],
            name="project",
        )(parity, to, current, faces, mortar)
        got = lax.all_to_all(send, "slab", 0, 0, tiled=True)
        placed = pl.pallas_call(
            place_kernel,
            out_shape=face,
            in_specs=[SMEM, SMEM, VMEM],
            out_specs=VMEM,
            name="place",
        )(parity, origin, got)
        add = lax.ppermute(placed, AXES, cross)
        add_inter = lax.ppermute(placed, AXES, cross_inter)
        add_same = lax.ppermute(placed, AXES, cross_same)
        current = solve(
            False,
            robin_step == ROBIN - 1,
            current,
            x_inter,
            x_same,
            inverse,
            add,
            add_inter,
            add_same,
        )
    current, arrived = current
    return current[None], arrived[None]


def solution(mesh):
    in_specs = (
        P("side", "slab", None, None),
        P("side", "slab", None, None),
        P("side", "slab", None, None),
        P("side", "slab", None),
        P("side", "slab", None, None),
        P("side", "slab"),
        P("side", "slab"),
    )
    out_specs = (P("side", "slab", None, None), P("side", "slab", None))
    return jax.shard_map(
        on_device, mesh=mesh, in_specs=in_specs, out_specs=out_specs, check_vma=False
    )
```

```python
import jax
import jax.numpy as jnp
from jax import lax
from jax.experimental import pallas as pl
from jax.experimental.pallas import tpu as pltpu
from jax.sharding import PartitionSpec as P

DEGREE = 4
ROBIN = 2
CAP = 3
SEND = CAP + 1
HALO = DEGREE - 1

cheb_low = 0.1
cheb_high = 2.0

AXES = ("side", "slab")
VMEM = pl.BlockSpec(memory_space=pltpu.VMEM)
SMEM = pl.BlockSpec(memory_space=pltpu.SMEM)


def cheb_weights():
    centre = (cheb_high + cheb_low) / 2.0
    half_width = (cheb_high - cheb_low) / 2.0
    ratio = centre / half_width
    weight_old = half_width / centre
    weights = [(0.0, 1.0 / centre)]
    for _ in range(DEGREE - 1):
        weight_new = 1.0 / (2.0 * ratio - weight_old)
        weights.append((weight_new * weight_old, 2.0 * weight_new / half_width))
        weight_old = weight_new
    return weights


def prepare_kernel(
    par_ref, src_ref, con_ref, rea_ref, gain_ref, beta_ref, gamma_ref, inter_ref, far_ref, same_ref, face_ref
):
    rows, ny, nz = src_ref.shape
    lanes = 128
    tiles = nz // lanes
    per_row = tiles * ny
    flip = par_ref[0] == 0
    chunk = lanes
    last_lane = lax.broadcasted_iota(jnp.int32, (chunk, lanes), 1) == lanes - 1
    base = HALO * per_row
    for row in range(rows):
        held = jnp.where(flip, rows - 1 - row, row)
        for tile in range(tiles):
            for part in range(ny // chunk):
                ys = pl.ds(part * chunk, chunk)
                zs = pl.ds(tile * lanes, lanes)
                con = con_ref[held, ys, zs]
                diag = 6.0 * con + rea_ref[held, ys, zs]
                if tile == tiles - 1:
                    gains = gain_ref[held, :, ys]
                    column = jnp.broadcast_to(gains, (chunk, chunk)).T
                    diag = diag + jnp.where(last_lane, column, 0.0)
                inverse = 1.0 / diag
                beta = src_ref[held, ys, zs] * inverse
                gamma = con * inverse
                at = tile * ny + part * chunk
                beta_ref[row, pl.ds(at, chunk), :] = beta
                gamma_ref[row, pl.ds(at, chunk), :] = gamma
                if row >= rows - HALO:
                    to = (row - (rows - HALO)) * per_row + at
                    inter_ref[pl.ds(to, chunk), :] = beta
                    if row == rows - HALO:
                        far_ref[pl.ds(at, chunk), :] = gamma
                    else:
                        inter_ref[pl.ds(base - per_row + to, chunk), :] = gamma
                if row < HALO:
                    to = row * per_row + at
                    same_ref[pl.ds(to, chunk), :] = beta
                    same_ref[pl.ds(base + to, chunk), :] = gamma
                if tile == tiles - 1:
                    block = row * (ny // chunk) + part
                    inverse_top = inverse.T[lanes - 1 :, :]
                    con_top = con.T[lanes - 1 :, :]
                    face_ref[0, pl.ds(block, 1), :] = con_top
                    face_ref[1, pl.ds(block, 1), :] = gains
                    far_ref[pl.ds(per_row + block, 1), :] = inverse_top
                    same_ref[pl.ds(2 * base + block, 1), :] = inverse_top


def solve_kernel(first, last, *refs):
    refs = list(refs)
    if last:
        par_ref = refs.pop(0)
    beta_ref, gamma_ref, inter_ref, same_ref = refs[:4]
    refs = refs[4:]
    if not first:
        x_ref, x_inter_ref, x_same_ref, own_far_ref, far_ref = refs[:5]
        add_ref, add_inter_ref, add_same_ref = refs[5:8]
        refs = refs[8:]
    out_ref = refs.pop(0)
    inc_ref = refs.pop(0) if last else None
    field, step, lift = refs
    rows = beta_ref.shape[0]
    lanes = 128
    tiles = 2
    ny = beta_ref.shape[1] // tiles
    per_row = tiles * ny
    pad = 8
    base = HALO * per_row
    chunk = 64
    parts = ny // chunk
    halves = ny // lanes
    weights = cheb_weights()
    lane = lax.broadcasted_iota(jnp.int32, (chunk, lanes), 1)
    first_lane, last_lane = lane == 0, lane == lanes - 1

    def static(which, row, at):
        if 0 <= row < rows:
            return (beta_ref, gamma_ref)[which][row, pl.ds(at, chunk), :]
        if row >= rows:
            ref, line = inter_ref, HALO + rows - 1 - row
            if which == 1 and line == 0:
                return far_ref[pl.ds(at, chunk), :]
            line -= which
        else:
            ref, line = same_ref, -1 - row
        return ref[pl.ds(which * base + line * per_row + at, chunk), :]

    zero = jnp.zeros((pad, lanes), jnp.float32)
    for buffer in range(2):
        for row in range(field.shape[1]):
            for tile in range(tiles):
                field[buffer, row, tile, pl.ds(0, pad), :] = zero
                field[buffer, row, tile, pl.ds(pad + ny, pad), :] = zero
    if not first:
        for row in range(-rows, 2 * rows):
            if 0 <= row < rows:
                ref, line = x_ref, row
            elif row >= rows:
                ref, line = x_inter_ref, 2 * rows - 1 - row
            else:
                ref, line = x_same_ref, -1 - row
            for tile in range(tiles):
                field[0, row + rows, tile, pl.ds(pad, ny), :] = ref[line, pl.ds(tile * ny, ny), :]
        wide = lax.broadcasted_iota(jnp.int32, (lanes, lanes), 1) == lanes - 1
        for row in range(-HALO, rows + HALO):
            if 0 <= row < rows:
                got, scale, at, line = add_ref, own_far_ref, per_row, row
            elif row >= rows:
                got, scale, at, line = add_inter_ref, far_ref, per_row, 2 * rows - 1 - row
            else:
                got, scale, at, line = add_same_ref, same_ref, 2 * base, -1 - row
            for half in range(halves):
                block = line * halves + half
                term = got[pl.ds(block, 1), :] * scale[pl.ds(at + block, 1), :]
                column = jnp.broadcast_to(term, (lanes, lanes)).T
                lift[row + HALO, pl.ds(half * lanes, lanes), :] = jnp.where(wide, column, 0.0)

    for sweep in range(DEGREE):
        reach = HALO - sweep
        now, later = sweep % 2, (sweep + 1) % 2
        for row in range(-reach, rows + reach):

            def body(part, carry, row=row, sweep=sweep, now=now, later=later):
                y0 = pl.multiple_of(part * chunk, chunk)
                keep, gain = weights[sweep]
                here = row + rows
                if first and sweep == 0:
                    for tile in range(tiles):
                        new = gain * static(0, row, tile * ny + y0)
                        step[row + HALO, tile, pl.ds(y0, chunk), :] = new
                        field[later, here, tile, pl.ds(pad + y0, chunk), :] = new
                    return carry
                centre = [field[now, here, t, pl.ds(pad + y0, chunk), :] for t in range(tiles)]
                ahead = [pltpu.roll(c, lanes - 1, 1) for c in centre]
                behind = [pltpu.roll(c, 1, 1) for c in centre]
                for tile in range(tiles):
                    x = centre[tile]
                    beside = field[now, here + 1, tile, pl.ds(pad + y0, chunk), :]
                    beside = beside + field[now, here - 1, tile, pl.ds(pad + y0, chunk), :]
                    beside = beside + field[now, here, tile, pl.ds(pad + y0 + 1, chunk), :]
                    beside = beside + field[now, here, tile, pl.ds(pad + y0 - 1, chunk), :]
                    above = ahead[tile + 1] if tile + 1 < tiles else 0.0
                    below = behind[tile - 1] if tile > 0 else 0.0
                    beside = beside + jnp.where(last_lane, above, ahead[tile])
                    beside = beside + jnp.where(first_lane, below, behind[tile])
                    beta = static(0, row, tile * ny + y0)
                    if not first and tile == tiles - 1:
                        beta = beta + lift[row + HALO, pl.ds(y0, chunk), :]
                    scaled = beta - x + static(1, row, tile * ny + y0) * beside
                    new = gain * scaled
                    if sweep > 0:
                        new = new + keep * step[row + HALO, tile, pl.ds(y0, chunk), :]
                    if sweep < DEGREE - 1:
                        step[row + HALO, tile, pl.ds(y0, chunk), :] = new
                        field[later, here, tile, pl.ds(pad + y0, chunk), :] = x + new
                    elif last:
                        line = jnp.where(par_ref[0] == 0, rows - 1 - row, row)
                        out_ref[line, pl.ds(y0, chunk), pl.ds(tile * lanes, lanes)] = x + new
                    else:
                        out_ref[row, pl.ds(tile * ny + y0, chunk), :] = x + new
                return carry

            lax.fori_loop(0, parts, body, 0, unroll=True)
    if last:
        for row in range(rows):
            line = jnp.where(par_ref[0] == 0, rows - 1 - row, row)
            for half in range(halves):
                inc_ref[pl.ds(line * halves + half, 1), :] = add_ref[pl.ds(row * halves + half, 1), :]


def project_kernel(par_ref, to_ref, x_ref, face_ref, mortar_ref, table_ref, send_ref, datum):
    rows = x_ref.shape[0]
    lanes = 128
    ny = x_ref.shape[1] // 2
    halves = ny // lanes
    blocks = rows * halves
    flip = par_ref[0] == 0
    send_ref[...] = jnp.zeros_like(send_ref)
    send_ref[pl.ds(CAP, table_ref.shape[0], stride=SEND), :] = table_ref[...]
    for row in range(rows):
        line = jnp.where(flip, rows - 1 - row, row)
        for half in range(halves):
            turned = x_ref[row, pl.ds(ny + half * lanes, lanes), :].T
            top = turned[lanes - 1 :, :]
            below = turned[lanes - 2 : lanes - 1, :]
            held = pl.ds(row * halves + half, 1)
            value = face_ref[1, held, :] * top - face_ref[0, held, :] * (top - below)
            datum[pl.ds(line * halves + half, 1), :] = value
    data = datum[...]
    for block in range(blocks):
        product = lax.dot_general(
            data,
            mortar_ref[block],
            (((1,), (1,)), ((), ())),
            precision=lax.Precision.HIGHEST,
            preferred_element_type=jnp.float32,
        )
        send_ref[pl.ds(to_ref[block], 1), :] = product[block : block + 1, :]


def place_kernel(par_ref, from_ref, got_ref, out_ref):
    blocks = out_ref.shape[0]
    halves = 2
    rows = blocks // halves
    flip = par_ref[0] == 0
    for row in range(rows):
        line = jnp.where(flip, rows - 1 - row, row)
        for half in range(halves):
            at = from_ref[line * halves + half]
            out_ref[pl.ds(row * halves + half, 1), :] = got_ref[pl.ds(at, 1), :]


def routes(count, swap_sides):
    same, inter = [], []
    for side in range(2):
        other = (1 - side if swap_sides else side) * count
        for low in range(count):
            me = side * count + low
            same.append((me, other + (low ^ 1)))
            near = low + 1 if low % 2 else low - 1
            if 0 <= near < count:
                inter.append((me, other + near))
    return inter, same


def on_device(source, conduct, reaction, robin_gain, mortar, dst_part, dst_slot):
    source, conduct, reaction, robin_gain = source[0], conduct[0], reaction[0], robin_gain[0]
    mortar, dst_part, dst_slot = mortar[0], dst_part[0], dst_slot[0]
    rows, ny, nz = source.shape
    blocks, lanes = mortar.shape[:2]
    count = lax.axis_size("slab")
    per_row = ny * nz // lanes
    parity = (lax.axis_index("slab") % 2).astype(jnp.int32).reshape(1)
    f32 = jnp.float32
    inter_route, same_route = routes(count, False)

    def exchange(inter, same):
        return lax.ppermute(inter, AXES, inter_route), lax.ppermute(same, AXES, same_route)

    rank = jnp.sum(
        jnp.tril(dst_part[:, None] == dst_part[None, :], -1).astype(jnp.int32), axis=1
    )
    to = dst_part * SEND + rank
    mine = (dst_part[:, None] == jnp.arange(count)[None, :])[:, :, None] & (
        rank[:, None] == jnp.arange(lanes)[None, :]
    )[:, None, :]
    table = jnp.sum(jnp.where(mine, dst_slot[:, None, None] + 1, 0), axis=0).astype(f32)

    def origins(table):
        row = jnp.arange(count)[:, None] * SEND + jnp.arange(lanes)[None, :]
        hit = table[None] == (jnp.arange(blocks) + 1).astype(f32)[:, None, None]
        return jnp.sum(jnp.where(hit, row[None], 0), axis=(1, 2)).astype(jnp.int32)

    cells = jax.ShapeDtypeStruct((rows, per_row, lanes), f32)
    packed = jax.ShapeDtypeStruct((2 * HALO * per_row + blocks, lanes), f32)
    near = jax.ShapeDtypeStruct(((2 * HALO - 1) * per_row, lanes), f32)
    rest = jax.ShapeDtypeStruct((per_row + blocks, lanes), f32)
    face = jax.ShapeDtypeStruct((blocks, lanes), f32)
    beta, gamma, inter, own_far, same, faces = pl.pallas_call(
        prepare_kernel,
        out_shape=(cells, cells, near, rest, packed, jax.ShapeDtypeStruct((2, blocks, lanes), f32)),
        in_specs=[SMEM] + [VMEM] * 4,
        out_specs=(VMEM,) * 6,
        name="prepare",
    )(parity, source, conduct, reaction, robin_gain[:, None, :])
    inter, same = exchange(inter, same)
    far = lax.ppermute(own_far, AXES, inter_route)

    def solve(first, last, *operands):
        scratch = [
            pltpu.VMEM((2, 3 * rows, 2, ny + 16, lanes), f32),
            pltpu.VMEM((rows + 2 * HALO, 2, ny, lanes), f32),
            pltpu.VMEM((rows + 2 * HALO, ny, lanes), f32),
        ]
        if last:
            out_shape = (jax.ShapeDtypeStruct((rows, ny, nz), f32), face)
            out_specs, lead, lead_specs = (VMEM, VMEM), (parity,), [SMEM]
        else:
            out_shape, out_specs, lead, lead_specs = cells, VMEM, (), []
        operands = (beta, gamma, inter, same) + operands
        return pl.pallas_call(
            lambda *refs: solve_kernel(first, last, *refs),
            out_shape=out_shape,
            in_specs=lead_specs + [VMEM] * len(operands),
            out_specs=out_specs,
            scratch_shapes=scratch,
            name="solve",
        )(*lead, *operands)

    cross_inter, cross_same = routes(count, True)
    cross = [(i, (i + count) % (2 * count)) for i in range(2 * count)]
    current = solve(True, False)
    for robin_step in range(ROBIN):
        x_inter, x_same = exchange(current, current)
        send = pl.pallas_call(
            project_kernel,
            out_shape=jax.ShapeDtypeStruct((count * SEND, lanes), f32),
            in_specs=[SMEM, SMEM, VMEM, VMEM, VMEM, VMEM],
            out_specs=VMEM,
            scratch_shapes=[pltpu.VMEM((blocks, lanes), f32)],
            name="project",
        )(parity, to, current, faces, mortar, table)
        got = lax.all_to_all(send, "slab", 0, 0, tiled=True)
        if robin_step == 0:
            origin = origins(got.reshape(count, SEND, lanes)[:, CAP])
        placed = pl.pallas_call(
            place_kernel,
            out_shape=face,
            in_specs=[SMEM, SMEM, VMEM],
            out_specs=VMEM,
            name="place",
        )(parity, origin, got)
        add = lax.ppermute(placed, AXES, cross)
        add_inter = lax.ppermute(placed, AXES, cross_inter)
        add_same = lax.ppermute(placed, AXES, cross_same)
        current = solve(
            False,
            robin_step == ROBIN - 1,
            current,
            x_inter,
            x_same,
            own_far,
            far,
            add,
            add_inter,
            add_same,
        )
    current, arrived = current
    return current[None], arrived[None]


def solution(mesh):
    in_specs = (
        P("side", "slab", None, None),
        P("side", "slab", None, None),
        P("side", "slab", None, None),
        P("side", "slab", None),
        P("side", "slab", None, None),
        P("side", "slab"),
        P("side", "slab"),
    )
    out_specs = (P("side", "slab", None, None), P("side", "slab", None))
    return jax.shard_map(
        on_device, mesh=mesh, in_specs=in_specs, out_specs=out_specs, check_vma=False
    )
```

```python
import jax
import jax.numpy as jnp
from jax import lax
from jax.experimental import pallas as pl
from jax.experimental.pallas import tpu as pltpu
from jax.sharding import PartitionSpec as P

DEGREE = 4
ROBIN = 2
CAP = 3
SEND = CAP + 1
HALO = DEGREE - 1

cheb_low = 0.1
cheb_high = 2.0

AXES = ("side", "slab")
VMEM = pl.BlockSpec(memory_space=pltpu.VMEM)
SMEM = pl.BlockSpec(memory_space=pltpu.SMEM)


def cheb_weights():
    centre = (cheb_high + cheb_low) / 2.0
    half_width = (cheb_high - cheb_low) / 2.0
    ratio = centre / half_width
    weight_old = half_width / centre
    weights = [(0.0, 1.0 / centre)]
    for _ in range(DEGREE - 1):
        weight_new = 1.0 / (2.0 * ratio - weight_old)
        weights.append((weight_new * weight_old, 2.0 * weight_new / half_width))
        weight_old = weight_new
    return weights


def prepare_kernel(
    par_ref, src_ref, con_ref, rea_ref, gain_ref, beta_ref, gamma_ref, inter_ref, far_ref, same_ref, face_ref
):
    rows, ny, nz = src_ref.shape
    lanes = 128
    tiles = nz // lanes
    per_row = tiles * ny
    flip = par_ref[0] == 0
    chunk = lanes
    last_lane = lax.broadcasted_iota(jnp.int32, (chunk, lanes), 1) == lanes - 1
    base = HALO * per_row
    for row in range(rows):
        held = jnp.where(flip, rows - 1 - row, row)
        for tile in range(tiles):
            for part in range(ny // chunk):
                ys = pl.ds(part * chunk, chunk)
                zs = pl.ds(tile * lanes, lanes)
                con = con_ref[held, ys, zs]
                diag = 6.0 * con + rea_ref[held, ys, zs]
                if tile == tiles - 1:
                    gains = jnp.where(flip, gain_ref[rows - 1 - row : rows - row, ys], gain_ref[row : row + 1, ys])
                    column = jnp.broadcast_to(gains, (chunk, chunk)).T
                    diag = diag + jnp.where(last_lane, column, 0.0)
                inverse = 1.0 / diag
                beta = src_ref[held, ys, zs] * inverse
                gamma = con * inverse
                at = tile * ny + part * chunk
                beta_ref[row, pl.ds(at, chunk), :] = beta
                gamma_ref[row, pl.ds(at, chunk), :] = gamma
                if row >= rows - HALO:
                    to = (row - (rows - HALO)) * per_row + at
                    inter_ref[pl.ds(to, chunk), :] = beta
                    if row == rows - HALO:
                        far_ref[pl.ds(at, chunk), :] = gamma
                    else:
                        inter_ref[pl.ds(base - per_row + to, chunk), :] = gamma
                if row < HALO:
                    to = row * per_row + at
                    same_ref[pl.ds(to, chunk), :] = beta
                    same_ref[pl.ds(base + to, chunk), :] = gamma
                if tile == tiles - 1:
                    block = row * (ny // chunk) + part
                    inverse_top = inverse.T[lanes - 1 :, :]
                    con_top = con.T[lanes - 1 :, :]
                    face_ref[0, pl.ds(block, 1), :] = con_top
                    face_ref[1, pl.ds(block, 1), :] = gains
                    far_ref[pl.ds(per_row + block, 1), :] = inverse_top
                    same_ref[pl.ds(2 * base + block, 1), :] = inverse_top


def solve_kernel(first, last, *refs):
    refs = list(refs)
    if last:
        par_ref = refs.pop(0)
    beta_ref, gamma_ref, inter_ref, same_ref = refs[:4]
    refs = refs[4:]
    if not first:
        x_ref, x_inter_ref, x_same_ref, own_far_ref, far_ref = refs[:5]
        add_ref, add_inter_ref, add_same_ref = refs[5:8]
        refs = refs[8:]
    out_ref = refs.pop(0)
    inc_ref = refs.pop(0) if last else None
    field, step, lift = refs
    rows = beta_ref.shape[0]
    lanes = 128
    tiles = 2
    ny = beta_ref.shape[1] // tiles
    per_row = tiles * ny
    pad = 8
    base = HALO * per_row
    chunk = 64
    parts = ny // chunk
    halves = ny // lanes
    weights = cheb_weights()
    lane = lax.broadcasted_iota(jnp.int32, (chunk, lanes), 1)
    first_lane, last_lane = lane == 0, lane == lanes - 1

    def static(which, row, at):
        if 0 <= row < rows:
            return (beta_ref, gamma_ref)[which][row, pl.ds(at, chunk), :]
        if row >= rows:
            ref, line = inter_ref, HALO + rows - 1 - row
            if which == 1 and line == 0:
                return far_ref[pl.ds(at, chunk), :]
            line -= which
        else:
            ref, line = same_ref, -1 - row
        return ref[pl.ds(which * base + line * per_row + at, chunk), :]

    zero = jnp.zeros((pad, lanes), jnp.float32)
    for buffer in range(2):
        for row in range(field.shape[1]):
            for tile in range(tiles):
                field[buffer, row, tile, pl.ds(0, pad), :] = zero
                field[buffer, row, tile, pl.ds(pad + ny, pad), :] = zero
    if not first:
        for row in range(-rows, 2 * rows):
            if 0 <= row < rows:
                ref, line = x_ref, row
            elif row >= rows:
                ref, line = x_inter_ref, 2 * rows - 1 - row
            else:
                ref, line = x_same_ref, -1 - row
            for tile in range(tiles):
                field[0, row + rows, tile, pl.ds(pad, ny), :] = ref[line, pl.ds(tile * ny, ny), :]
        wide = lax.broadcasted_iota(jnp.int32, (lanes, lanes), 1) == lanes - 1
        for row in range(-HALO, rows + HALO):
            if 0 <= row < rows:
                got, scale, at, line = add_ref, own_far_ref, per_row, row
            elif row >= rows:
                got, scale, at, line = add_inter_ref, far_ref, per_row, 2 * rows - 1 - row
            else:
                got, scale, at, line = add_same_ref, same_ref, 2 * base, -1 - row
            for half in range(halves):
                block = line * halves + half
                term = got[pl.ds(block, 1), :] * scale[pl.ds(at + block, 1), :]
                column = jnp.broadcast_to(term, (lanes, lanes)).T
                lift[row + HALO, pl.ds(half * lanes, lanes), :] = jnp.where(wide, column, 0.0)

    for sweep in range(DEGREE):
        reach = HALO - sweep
        now, later = sweep % 2, (sweep + 1) % 2
        for row in range(-reach, rows + reach):

            def body(part, carry, row=row, sweep=sweep, now=now, later=later):
                y0 = pl.multiple_of(part * chunk, chunk)
                keep, gain = weights[sweep]
                here = row + rows
                if first and sweep == 0:
                    for tile in range(tiles):
                        new = gain * static(0, row, tile * ny + y0)
                        step[row + HALO, tile, pl.ds(y0, chunk), :] = new
                        field[later, here, tile, pl.ds(pad + y0, chunk), :] = new
                    return carry
                centre = [field[now, here, t, pl.ds(pad + y0, chunk), :] for t in range(tiles)]
                ahead = [pltpu.roll(c, lanes - 1, 1) for c in centre]
                behind = [pltpu.roll(c, 1, 1) for c in centre]
                for tile in range(tiles):
                    x = centre[tile]
                    beside = field[now, here + 1, tile, pl.ds(pad + y0, chunk), :]
                    beside = beside + field[now, here - 1, tile, pl.ds(pad + y0, chunk), :]
                    beside = beside + field[now, here, tile, pl.ds(pad + y0 + 1, chunk), :]
                    beside = beside + field[now, here, tile, pl.ds(pad + y0 - 1, chunk), :]
                    above = ahead[tile + 1] if tile + 1 < tiles else 0.0
                    below = behind[tile - 1] if tile > 0 else 0.0
                    beside = beside + jnp.where(last_lane, above, ahead[tile])
                    beside = beside + jnp.where(first_lane, below, behind[tile])
                    beta = static(0, row, tile * ny + y0)
                    if not first and tile == tiles - 1:
                        beta = beta + lift[row + HALO, pl.ds(y0, chunk), :]
                    scaled = beta - x + static(1, row, tile * ny + y0) * beside
                    new = gain * scaled
                    if sweep > 0:
                        new = new + keep * step[row + HALO, tile, pl.ds(y0, chunk), :]
                    if sweep < DEGREE - 1:
                        step[row + HALO, tile, pl.ds(y0, chunk), :] = new
                        field[later, here, tile, pl.ds(pad + y0, chunk), :] = x + new
                    elif last:
                        line = jnp.where(par_ref[0] == 0, rows - 1 - row, row)
                        out_ref[line, pl.ds(y0, chunk), pl.ds(tile * lanes, lanes)] = x + new
                    else:
                        out_ref[row, pl.ds(tile * ny + y0, chunk), :] = x + new
                return carry

            lax.fori_loop(0, parts, body, 0, unroll=True)
    if last:
        for row in range(rows):
            line = jnp.where(par_ref[0] == 0, rows - 1 - row, row)
            for half in range(halves):
                inc_ref[pl.ds(line * halves + half, 1), :] = add_ref[pl.ds(row * halves + half, 1), :]


def split(value):
    high = value.astype(jnp.bfloat16)
    return high, (value - high.astype(jnp.float32)).astype(jnp.bfloat16)


def times(data, matrix):
    return lax.dot_general(
        data, matrix, (((1,), (1,)), ((), ())), preferred_element_type=jnp.float32
    )


def project_kernel(par_ref, to_ref, x_ref, face_ref, mortar_ref, table_ref, send_ref, datum):
    rows = x_ref.shape[0]
    lanes = 128
    ny = x_ref.shape[1] // 2
    halves = ny // lanes
    blocks = rows * halves
    flip = par_ref[0] == 0
    send_ref[...] = jnp.zeros_like(send_ref)
    send_ref[pl.ds(CAP, table_ref.shape[0], stride=SEND), :] = table_ref[...]
    for row in range(rows):
        line = jnp.where(flip, rows - 1 - row, row)
        for half in range(halves):
            turned = x_ref[row, pl.ds(ny + half * lanes, lanes), :].T
            top = turned[lanes - 1 :, :]
            below = turned[lanes - 2 : lanes - 1, :]
            held = pl.ds(row * halves + half, 1)
            value = face_ref[1, held, :] * top - face_ref[0, held, :] * (top - below)
            datum[pl.ds(line * halves + half, 1), :] = value
    data_high, data_low = split(datum[...])
    data = jnp.concatenate([data_high, data_low], axis=0)
    for block in range(blocks):
        high, low = split(mortar_ref[block])
        by_high, by_low = times(data, high), times(data, low)
        product = by_high[:blocks] + (by_high[blocks:] + by_low[:blocks]) + by_low[blocks:]
        send_ref[pl.ds(to_ref[block], 1), :] = product[block : block + 1, :]


def place_kernel(par_ref, from_ref, got_ref, out_ref):
    blocks = out_ref.shape[0]
    halves = 2
    rows = blocks // halves
    flip = par_ref[0] == 0
    for row in range(rows):
        line = jnp.where(flip, rows - 1 - row, row)
        for half in range(halves):
            at = from_ref[line * halves + half]
            out_ref[pl.ds(row * halves + half, 1), :] = got_ref[pl.ds(at, 1), :]


def routes(count, swap_sides):
    same, inter = [], []
    for side in range(2):
        other = (1 - side if swap_sides else side) * count
        for low in range(count):
            me = side * count + low
            same.append((me, other + (low ^ 1)))
            near = low + 1 if low % 2 else low - 1
            if 0 <= near < count:
                inter.append((me, other + near))
    return inter, same


def on_device(source, conduct, reaction, robin_gain, mortar, dst_part, dst_slot):
    source, conduct, reaction, robin_gain = source[0], conduct[0], reaction[0], robin_gain[0]
    mortar, dst_part, dst_slot = mortar[0], dst_part[0], dst_slot[0]
    rows, ny, nz = source.shape
    blocks, lanes = mortar.shape[:2]
    count = lax.axis_size("slab")
    per_row = ny * nz // lanes
    parity = (lax.axis_index("slab") % 2).astype(jnp.int32).reshape(1)
    f32 = jnp.float32
    inter_route, same_route = routes(count, False)

    def exchange(inter, same):
        return lax.ppermute(inter, AXES, inter_route), lax.ppermute(same, AXES, same_route)

    rank = jnp.sum(
        jnp.tril(dst_part[:, None] == dst_part[None, :], -1).astype(jnp.int32), axis=1
    )
    to = dst_part * SEND + rank
    mine = (dst_part[:, None] == jnp.arange(count)[None, :])[:, :, None] & (
        rank[:, None] == jnp.arange(lanes)[None, :]
    )[:, None, :]
    table = jnp.sum(jnp.where(mine, dst_slot[:, None, None] + 1, 0), axis=0).astype(f32)

    def origins(table):
        row = jnp.arange(count)[:, None] * SEND + jnp.arange(lanes)[None, :]
        hit = table[None] == (jnp.arange(blocks) + 1).astype(f32)[:, None, None]
        return jnp.sum(jnp.where(hit, row[None], 0), axis=(1, 2)).astype(jnp.int32)

    cells = jax.ShapeDtypeStruct((rows, per_row, lanes), f32)
    packed = jax.ShapeDtypeStruct((2 * HALO * per_row + blocks, lanes), f32)
    near = jax.ShapeDtypeStruct(((2 * HALO - 1) * per_row, lanes), f32)
    rest = jax.ShapeDtypeStruct((per_row + blocks, lanes), f32)
    face = jax.ShapeDtypeStruct((blocks, lanes), f32)
    beta, gamma, inter, own_far, same, faces = pl.pallas_call(
        prepare_kernel,
        out_shape=(cells, cells, near, rest, packed, jax.ShapeDtypeStruct((2, blocks, lanes), f32)),
        in_specs=[SMEM] + [VMEM] * 4,
        out_specs=(VMEM,) * 6,
        name="prepare",
    )(parity, source, conduct, reaction, robin_gain)
    inter, same = exchange(inter, same)
    far = lax.ppermute(own_far, AXES, inter_route)

    def solve(first, last, *operands):
        scratch = [
            pltpu.VMEM((2, 3 * rows, 2, ny + 16, lanes), f32),
            pltpu.VMEM((rows + 2 * HALO, 2, ny, lanes), f32),
            pltpu.VMEM((rows + 2 * HALO, ny, lanes), f32),
        ]
        if last:
            out_shape = (jax.ShapeDtypeStruct((rows, ny, nz), f32), face)
            out_specs, lead, lead_specs = (VMEM, VMEM), (parity,), [SMEM]
        else:
            out_shape, out_specs, lead, lead_specs = cells, VMEM, (), []
        operands = (beta, gamma, inter, same) + operands
        return pl.pallas_call(
            lambda *refs: solve_kernel(first, last, *refs),
            out_shape=out_shape,
            in_specs=lead_specs + [VMEM] * len(operands),
            out_specs=out_specs,
            scratch_shapes=scratch,
            name="solve",
        )(*lead, *operands)

    cross_inter, cross_same = routes(count, True)
    cross = [(i, (i + count) % (2 * count)) for i in range(2 * count)]
    current = solve(True, False)
    for robin_step in range(ROBIN):
        x_inter, x_same = exchange(current, current)
        send = pl.pallas_call(
            project_kernel,
            out_shape=jax.ShapeDtypeStruct((count * SEND, lanes), f32),
            in_specs=[SMEM, SMEM, VMEM, VMEM, VMEM, VMEM],
            out_specs=VMEM,
            scratch_shapes=[pltpu.VMEM((blocks, lanes), f32)],
            name="project",
        )(parity, to, current, faces, mortar, table)
        got = lax.all_to_all(send, "slab", 0, 0, tiled=True)
        if robin_step == 0:
            origin = origins(got.reshape(count, SEND, lanes)[:, CAP])
        placed = pl.pallas_call(
            place_kernel,
            out_shape=face,
            in_specs=[SMEM, SMEM, VMEM],
            out_specs=VMEM,
            name="place",
        )(parity, origin, got)
        add = lax.ppermute(placed, AXES, cross)
        add_inter = lax.ppermute(placed, AXES, cross_inter)
        add_same = lax.ppermute(placed, AXES, cross_same)
        current = solve(
            False,
            robin_step == ROBIN - 1,
            current,
            x_inter,
            x_same,
            own_far,
            far,
            add,
            add_inter,
            add_same,
        )
    current, arrived = current
    return current[None], arrived[None]


def solution(mesh):
    in_specs = (
        P("side", "slab", None, None),
        P("side", "slab", None, None),
        P("side", "slab", None, None),
        P("side", "slab", None),
        P("side", "slab", None, None),
        P("side", "slab"),
        P("side", "slab"),
    )
    out_specs = (P("side", "slab", None, None), P("side", "slab", None))
    return jax.shard_map(
        on_device, mesh=mesh, in_specs=in_specs, out_specs=out_specs, check_vma=False
    )
```
